512 devices in a mesh: video: 16 (over x, z_hi, core), tm: 32 (over y, z_lo).
Axes of the slice: x: 4, y: 8, z: 8 (z_hi: 2, z_lo: 4; z = z_hi * 4 + z_lo), core: 2. Of those that a mesh axis runs over, the one named last changes fastest.
Arguments:
- frames: bfloat16 [512, 28, 28, 704], P(('video', 'tm')), parts along dimension 0, may hold values from -6 to 6
- clip_cut: int32 [512], P(('video', 'tm')), parts along dimension 0, may hold values 0 or 1
- space_kernel: float32 [49, 704], replicated, may hold values from -0.8 to 0.8
- time_kernel: float32 [3, 704], replicated, may hold values from -3 to 3
- conv_bias: float32 [704], replicated, may hold values from -3 to 3
- norm_gain: float32 [704], replicated, may hold values from 0.5 to 1.5
- norm_bias: float32 [704], replicated, may hold values from -3 to 3
- up_weight: bfloat16 [704, 2816], P(None, 'tm'), may hold values from -0.21875 to 0.21875
- up_bias: float32 [2816], replicated, may hold values from -3 to 3
- grn_gamma: float32 [2816], replicated, may hold values from -3 to 3
- grn_beta: float32 [2816], replicated, may hold values from -3 to 3
- down_weight: bfloat16 [2816, 704], P('tm'), may hold values from -0.109375 to 0.109375
- down_bias: float32 [704], replicated, may hold values from -3 to 3
Outputs:
- block_out: bfloat16 [512, 28, 28, 704], P(('video', 'tm')), parts along dimension 0
The draws below stay inside these ranges and needn't reach their ends.
There are 16 independent parts, one for each index of `video`. The reference program is written for one: setup_inputs(seed, part) draws one part's arguments, and reference() takes and returns one part's arrays. A program takes and returns all parts, laid end to end along the dimension named above; an argument that names none is the same for every part. Nothing has to cross between parts.
All inputs are finite; a program needn't handle non-finite values. No bound on the sum of `clip_cut` on one device may be relied on, other than what follows from the above.
Results may differ from the reference program's by a relative error of at most 0.0054.
Values may be sent and summed in bfloat16 or wider, within the bound.
No kernel may reach another device: no remote copies, remote signals or barrier semaphores. Data moves between devices by JAX's collectives and lax.ppermute only.
A program may use at most 64 MiB of HBM per device.

```python
import jax
import jax.numpy as jnp
from jax import lax

C = 704
HID = 2816
H = 28
W = 28
FRAMES = 32


def set_ends(values, rng, smallest, top_value):
    extent = values.shape
    place = [jax.random.randint(jax.random.fold_in(rng, axis), (), 0, extent[axis]) for axis in range(len(extent))]
    values = values.at[tuple(place)].set(smallest)
    longest = extent.index(max(extent))
    place[longest] = (place[longest] + 1) % extent[longest]
    return values.at[tuple(place)].set(top_value)


def levels(rng, dims, split, least, top_value):
    gain = 1.0
    for axis_at, parts in split:
        steps = jax.random.uniform(jax.random.fold_in(jax.random.fold_in(rng, 6), axis_at), (parts,), jnp.float32, least / len(split), top_value / len(split))
        gain = gain * jnp.repeat(jnp.exp(steps), dims[axis_at] // parts).reshape((-1,) + (1,) * (len(dims) - 1 - axis_at))
    return gain


def centred(key, shape, width, bound, split=(), kind=jnp.bfloat16):
    level = levels(key, shape, split, -0.22, 0.18) if split else 1.0
    drawn = jax.random.normal(key, shape, jnp.float32) * width * level
    return jnp.minimum(jnp.maximum(drawn, -bound), bound).astype(kind)


def setup_inputs(seed: int = 0, part: int = 0) -> dict:
    streams_of = jax.random.split(jax.random.key(seed), 14)
    part_keys = jax.random.split(jax.random.fold_in(streams_of[13], part), 14)
    return {
        "frames": centred(part_keys[0], (FRAMES, H, W, C), 1.0, 6.0, ((0, 32),)),
        "clip_cut": set_ends((jax.random.randint(part_keys[1], (FRAMES,), 0, 4) < 1).astype(jnp.int32), jax.random.fold_in(part_keys[1], 1), 0, 1),
        "space_kernel": centred(streams_of[2], (49, C), 0.14, 0.8, (), jnp.float32),
        "time_kernel": centred(streams_of[3], (3, C), 0.6, 3.0, (), jnp.float32),
        "conv_bias": centred(streams_of[4], (C,), 0.5, 3.0, (), jnp.float32),
        "norm_gain": jnp.clip(jax.random.uniform(streams_of[5], (C,), jnp.float32, 0.5, 1.5), 0.5, 1.5),
        "norm_bias": centred(streams_of[6], (C,), 0.5, 3.0, (), jnp.float32),
        "up_weight": centred(streams_of[7], (C, HID), C ** -0.5, 0.21875, ((1, 32),)),
        "up_bias": centred(streams_of[8], (HID,), 0.5, 3.0, (), jnp.float32),
        "grn_gamma": centred(streams_of[9], (HID,), 0.5, 3.0, (), jnp.float32),
        "grn_beta": centred(streams_of[10], (HID,), 0.5, 3.0, (), jnp.float32),
        "down_weight": centred(streams_of[11], (HID, C), HID ** -0.5, 0.109375, ((0, 32),)),
        "down_bias": centred(streams_of[12], (C,), 0.5, 3.0, (), jnp.float32),
    }


def space_time(frames, prev_side, next_side, space_kernel, time_kernel, conv_bias):
    padded = jnp.pad(frames, ((0, 0), (3, 3), (3, 3), (0, 0)))
    total = jnp.zeros(frames.shape, jnp.float32)
    for row_off in range(7):
        for col_off in range(7):
            window = padded[:, row_off:row_off + frames.shape[1], col_off:col_off + frames.shape[2], :]
            total = total + window.astype(jnp.float32) * space_kernel[7 * row_off + col_off]
    total = total + time_kernel[0] * prev_side.astype(jnp.float32)
    total = total + time_kernel[1] * frames.astype(jnp.float32)
    total = total + time_kernel[2] * next_side.astype(jnp.float32)
    return total + conv_bias

def layer_norm(conv, norm_gain, norm_bias):
    mean_val = lax.optimization_barrier(jnp.mean(conv, axis=-1, keepdims=True))
    centered = conv - mean_val
    var_val = lax.optimization_barrier(jnp.mean(centered * centered, axis=-1, keepdims=True))
    return (centered / jnp.sqrt(var_val + 1e-06) * norm_gain + norm_bias).astype(jnp.bfloat16)

def response_norm(hidden, grn_gamma, grn_beta):
    hid32 = hidden.astype(jnp.float32)
    energy = jnp.sqrt(lax.optimization_barrier(jnp.sum(hid32 * hid32, axis=0)))
    ratio = energy / (jnp.mean(energy) + 1e-06)
    return (grn_gamma * hid32 * ratio + grn_beta + hid32).astype(jnp.bfloat16)

def reference(frames, clip_cut, space_kernel, time_kernel, conv_bias, norm_gain, norm_bias, up_weight, up_bias, grn_gamma, grn_beta, down_weight, down_bias):
    keep = (1 - clip_cut).astype(jnp.bfloat16)[:, None, None, None]
    zero_frame = jnp.zeros_like(frames[:1])
    prev_side = jnp.concatenate([zero_frame, frames[:-1]], axis=0) * keep
    masked = frames * keep
    next_side = jnp.concatenate([masked[1:], zero_frame], axis=0)

    def one_frame(inputs):
        frame, prev_one, next_one = inputs
        conv = space_time(frame[None], prev_one[None], next_one[None], space_kernel, time_kernel, conv_bias)[0]
        rows = conv.reshape(-1, conv.shape[-1])
        normed = layer_norm(rows, norm_gain, norm_bias)
        hidden = jax.nn.gelu(jnp.dot(normed, up_weight, preferred_element_type=jnp.float32) + up_bias, approximate=False).astype(jnp.bfloat16)
        grn = response_norm(hidden, grn_gamma, grn_beta)
        result = jnp.dot(grn, down_weight, preferred_element_type=jnp.float32) + down_bias + frame.reshape(rows.shape).astype(jnp.float32)
        return result.astype(jnp.bfloat16).reshape(frame.shape)
    return lax.map(one_frame, (frames, prev_side, next_side))
```

```python
import jax
import jax.numpy as jnp
from jax import lax
from jax.experimental import pallas as pl
from jax.experimental.pallas import tpu as pltpu
from jax.sharding import PartitionSpec as P

C, HID, H, W = 704, 2816, 28, 28
PIX = H * W
LANES = 128
CHUNKS = 6
HALF = 384
SHARD = 88
ROWS4 = 4 * SHARD
VMEM = 56 * 1024 * 1024
UP_OFFSETS = ((0, 1, 7, 2), (4, 5, 3, 6))
DOWN_OFFSETS = ((2, 7, 1, 0), (6, 3, 5, 4))

vmem_spec = pl.BlockSpec(memory_space=pltpu.VMEM)
smem_spec = pl.BlockSpec(memory_space=pltpu.SMEM)
any_spec = pl.BlockSpec(memory_space=pl.ANY)


def place():
    v = lax.axis_index("video")
    t = lax.axis_index("tm")
    return v // 4, v % 2, t // 4, t % 4


def pick(table, index):
    value = jnp.int32(table[0])
    for k in range(1, len(table)):
        value = jnp.where(index == k, jnp.int32(table[k]), value)
    return value


def permute(value, source_of):
    pairs = []
    for x in range(4):
        for zh in range(2):
            for c in range(2):
                for y in range(8):
                    for zl in range(4):
                        src = source_of(x, zh, c, y, zl)
                        if src is None:
                            continue
                        pairs.append((flat(*src), flat(x, zh, c, y, zl)))
    return lax.ppermute(value, ("video", "tm"), pairs)


def flat(x, zh, c, y, zl):
    return ((x * 2 + zh) * 2 + c) * 32 + y * 4 + zl


def from_frame(by):
    def source_of(x, zh, c, y, zl):
        t = y * 4 + zl + by
        return (x, zh, c, t // 4, t % 4) if 0 <= t < 32 else None

    return source_of


def widen(value):
    if value.shape[-1] == LANES:
        return value
    zeros = jnp.zeros(value.shape[:-1] + (LANES - value.shape[-1],), value.dtype)
    return jnp.concatenate([value, zeros], axis=-1)


def lanes(chunk):
    return slice(chunk * LANES, min((chunk + 1) * LANES, C))


def flatten_kernel(clip_ref, x_ref, flat_ref, masked_ref):
    keep = (1 - clip_ref[0]).astype(jnp.float32)
    for g in range(7):
        rows = jnp.concatenate([x_ref[4 * g + r].astype(jnp.float32) for r in range(4)], axis=0)
        flat_ref[112 * g : 112 * (g + 1), :] = rows.astype(jnp.bfloat16)
        masked_ref[112 * g : 112 * (g + 1), :] = (rows * keep).astype(jnp.bfloat16)


def flatten(clip, frame):
    out = jax.ShapeDtypeStruct((PIX, C), jnp.bfloat16)
    return pl.pallas_call(
        flatten_kernel,
        out_shape=(out, out),
        in_specs=[smem_spec, vmem_spec],
        out_specs=(vmem_spec, vmem_spec),
        compiler_params=pltpu.CompilerParams(vmem_limit_bytes=VMEM),
        name="flatten",
    )(clip, frame)


def conv_kernel(first, count, x_ref, k_ref, t_ref, b_ref, o_ref, xp, kb, bb):
    xp[...] = jnp.zeros_like(xp)
    for n in range(count):
        part = lanes(first + n)
        for i in range(H):
            xp[n, 3 + i, 3:31, :] = widen(x_ref[i, :, part].astype(jnp.float32))
        for tap in range(49):
            row = widen(k_ref[tap : tap + 1, part])
            if tap == 24:
                row = row + widen(t_ref[1:2, part])
            kb[n, tap] = jnp.broadcast_to(row, (8, LANES))
        bb[n] = jnp.broadcast_to(widen(b_ref[:, part]), (8, LANES))

    def body(step, carry):
        n = step // 7
        g = step % 7
        done = [[None] * 4 for _ in range(4)]
        for jb in range(4):
            acc = [bb[n]] * 4
            for b in range(7):
                xs = [xp[n, 4 * g + q, 8 * jb + b : 8 * jb + b + 8, :] for q in range(10)]
                for a in range(7):
                    kv = kb[n, 7 * a + b]
                    for r in range(4):
                        acc[r] = acc[r] + kv * xs[r + a]
            for r in range(4):
                done[r][jb] = acc[r] if jb < 3 else acc[r][:4]
        rows = jnp.concatenate([done[r][jb] for r in range(4) for jb in range(4)], axis=0)
        o_ref[n, pl.ds(pl.multiple_of(112 * g, 8), 112), :] = rows
        return carry

    lax.fori_loop(0, 7 * count, body, 0)


def conv(first, count, frame, space_kernel, time_kernel, conv_bias):
    return pl.pallas_call(
        lambda *refs: conv_kernel(first, count, *refs),
        out_shape=jax.ShapeDtypeStruct((count, PIX, LANES), jnp.float32),
        in_specs=[vmem_spec] * 4,
        out_specs=vmem_spec,
        scratch_shapes=[
            pltpu.VMEM((count, 34, 40, LANES), jnp.float32),
            pltpu.VMEM((count, 49, 8, LANES), jnp.float32),
            pltpu.VMEM((count, 8, LANES), jnp.float32),
        ],
        compiler_params=pltpu.CompilerParams(vmem_limit_bytes=VMEM),
        name="conv",
    )(frame, space_kernel, time_kernel, conv_bias)


def order_kernel(*refs):
    _, _, _, zl = place()
    blocks, (up_ref, down_ref) = refs[:4], refs[4:]
    for r in range(4):
        up_ref[zl ^ r] = blocks[r][0]
        down_ref[zl ^ r] = blocks[r][1]


def order(blocks):
    out = jax.ShapeDtypeStruct((4, SHARD, HALF), jnp.bfloat16)
    return pl.pallas_call(
        order_kernel,
        out_shape=(out, out),
        in_specs=[vmem_spec] * 4,
        out_specs=(vmem_spec, vmem_spec),
        compiler_params=pltpu.CompilerParams(vmem_limit_bytes=VMEM),
        name="order",
    )(*blocks)


def block_copies(offsets, own, other, weight, sems):
    x, core, y, _ = place()
    copies = []
    for step in range(4):
        for side in range(2):
            row = ((y + pick(offsets[side], (x + step) % 4)) % 8) * ROWS4
            for half, refs in ((core, own), (1 - core, other)):
                copies.append(
                    pltpu.make_async_copy(
                        refs[step].at[side],
                        weight.at[half, pl.ds(pl.multiple_of(row, 32), ROWS4), :],
                        sems.at[len(copies)],
                    )
                )
    return copies


def up_kernel(clip_ref, *refs):
    (c0_ref, c1_ref, prev_ref, next_ref, t_ref, gain_ref, nbias_ref, ubias_ref) = refs[:8]
    own, other = refs[8:12], refs[12:16]
    hid_ref, energy_ref, weight, normed, sems = refs[16:]
    copies = block_copies(UP_OFFSETS, own, other, weight, sems)
    for copy in copies:
        copy.start()
    keep = (1 - clip_ref[0]).astype(jnp.float32)

    def norm_rows(step, carry):
        rows = pl.ds(pl.multiple_of(step * 16, 16), 16)
        parts = []
        for n in range(CHUNKS):
            part = lanes(n)
            base = c0_ref[n, rows, :] if n < 3 else c1_ref[n - 3, rows, :]
            before = widen(prev_ref[rows, part].astype(jnp.float32)) * (widen(t_ref[0:1, part]) * keep)
            after = widen(next_ref[rows, part].astype(jnp.float32)) * widen(t_ref[2:3, part])
            parts.append(base + before + after)
        total = parts[0]
        for n in range(1, CHUNKS):
            total = total + parts[n]
        mean = jnp.sum(total, axis=-1, keepdims=True) * (1.0 / C)
        parts = [p - mean for p in parts]
        lane = lax.broadcasted_iota(jnp.int32, parts[-1].shape, 1)
        parts[-1] = jnp.where(lane < C - 5 * LANES, parts[-1], 0.0)
        total = parts[0] * parts[0]
        for n in range(1, CHUNKS):
            total = total + parts[n] * parts[n]
        var = jnp.sum(total, axis=-1, keepdims=True) * (1.0 / C)
        scale = lax.rsqrt(var + 1e-06)
        for n in range(CHUNKS):
            value = parts[n] * scale * widen(gain_ref[:, lanes(n)]) + widen(nbias_ref[:, lanes(n)])
            normed[rows, n * LANES : (n + 1) * LANES] = value.astype(jnp.bfloat16)
        return carry

    lax.fori_loop(0, PIX // 16, norm_rows, 0)
    for copy in copies:
        copy.wait()

    def units(step, carry):
        cols = pl.ds(pl.multiple_of(step * 256, 256), 256)
        dims = (((1,), (1,)), ((), ()))
        value = lax.dot_general(
            normed[:, :HALF], weight[0, cols, :], dims, preferred_element_type=jnp.float32
        ) + lax.dot_general(
            normed[:, HALF:], weight[1, cols, :], dims, preferred_element_type=jnp.float32
        )
        value = value + ubias_ref[:, cols]
        hid = (0.5 * value * (1.0 + lax.erf(value * 0.7071067811865476))).astype(jnp.bfloat16)
        hid_ref[:, cols] = hid
        wide = hid.astype(jnp.float32)
        energy_ref[:, cols] = jnp.sum(wide * wide, axis=0, keepdims=True)
        return carry

    lax.fori_loop(0, HID // 256, units, 0)


def up(clip, conv0, conv1, prev, nxt, time_kernel, gain, nbias, ubias, own, other):
    return pl.pallas_call(
        up_kernel,
        out_shape=(
            jax.ShapeDtypeStruct((PIX, HID), jnp.bfloat16),
            jax.ShapeDtypeStruct((1, HID), jnp.float32),
        ),
        in_specs=[smem_spec] + [vmem_spec] * 8 + [any_spec] * 8,
        out_specs=(vmem_spec, vmem_spec),
        scratch_shapes=[
            pltpu.VMEM((2, HID, HALF), jnp.bfloat16),
            pltpu.VMEM((PIX, CHUNKS * LANES), jnp.bfloat16),
            pltpu.SemaphoreType.DMA((16,)),
        ],
        compiler_params=pltpu.CompilerParams(vmem_limit_bytes=VMEM),
        name="up",
    )(clip, conv0, conv1, prev, nxt, time_kernel, gain, nbias, ubias, *own, *other)


def down_kernel(hid_ref, energy_ref, gamma_ref, beta_ref, dbias_ref, flat_ref, *refs):
    own, other = refs[:4], refs[4:8]
    out_ref, weight, grn, sums, sems = refs[8:]
    copies = block_copies(DOWN_OFFSETS, own, other, weight, sems)
    for copy in copies:
        copy.start()
    energy = jnp.sqrt(energy_ref[...])
    ratio = energy / (jnp.sum(energy, axis=1, keepdims=True) * (1.0 / HID) + 1e-06)
    grow = gamma_ref[...] * ratio + 1.0

    def scale(step, carry):
        rows = pl.ds(pl.multiple_of(step * 16, 16), 16)
        grn[rows, :] = (hid_ref[rows, :].astype(jnp.float32) * grow + beta_ref[...]).astype(jnp.bfloat16)
        return carry

    lax.fori_loop(0, PIX // 16, scale, 0)
    for copy in copies:
        copy.wait()
    for half in range(2):
        width = min(HALF, C - half * HALF)
        cols = slice(half * HALF, half * HALF + width)
        value = jnp.dot(grn[...], weight[half], preferred_element_type=jnp.float32)
        sums[:, cols] = value[:, :width]
    for g in range(7):
        rows = slice(112 * g, 112 * (g + 1))
        value = sums[rows, :] + dbias_ref[...] + flat_ref[rows, :].astype(jnp.float32)
        for r in range(4):
            out_ref[4 * g + r] = value[28 * r : 28 * (r + 1)].astype(jnp.bfloat16)


def down(hid, energy, gamma, beta, dbias, flat_frame, own, other):
    return pl.pallas_call(
        down_kernel,
        out_shape=jax.ShapeDtypeStruct((H, W, C), jnp.bfloat16),
        in_specs=[vmem_spec] * 6 + [any_spec] * 8,
        out_specs=vmem_spec,
        scratch_shapes=[
            pltpu.VMEM((2, HID, HALF), jnp.bfloat16),
            pltpu.VMEM((PIX, HID), jnp.bfloat16),
            pltpu.VMEM((PIX, C), jnp.float32),
            pltpu.SemaphoreType.DMA((16,)),
        ],
        compiler_params=pltpu.CompilerParams(vmem_limit_bytes=VMEM),
        name="down",
    )(hid, energy, gamma, beta, dbias, flat_frame, *own, *other)


def spread_z(up_weight, down_weight):
    core = lax.axis_index("video") % 2
    both = jnp.stack([up_weight.T, down_weight])
    both = jnp.pad(both, ((0, 0), (0, 0), (0, 2 * HALF - C)))
    mine = lax.dynamic_slice(both, (0, 0, core * HALF), (2, SHARD, HALF))
    blocks = [mine]
    for r in range(1, 4):
        blocks.append(permute(mine, lambda x, zh, c, y, zl: (x, zh, c, y, zl ^ r)))
    return order(blocks)


def spread_y(block, offsets):
    block = block.reshape(ROWS4, HALF)
    sides = [
        permute(block, lambda x, zh, c, y, zl: (x, zh, c, (y + side[x]) % 8, zl)) for side in offsets
    ]
    return jnp.stack(sides)


def spread_x(block):
    return [permute(block, lambda x, zh, c, y, zl: ((x + by) % 4, zh, c, y, zl)) for by in range(1, 4)]


def swap_core(block):
    return permute(block, lambda x, zh, c, y, zl: (x, zh, 1 - c, y, zl))


def per_device(
    frames,
    clip_cut,
    space_kernel,
    time_kernel,
    conv_bias,
    norm_gain,
    norm_bias,
    up_weight,
    up_bias,
    grn_gamma,
    grn_beta,
    down_weight,
    down_bias,
):
    frame = frames[0]
    row = lambda value: value[None]
    up4, down4 = spread_z(up_weight, down_weight)
    flat_frame, masked = flatten(clip_cut, frame)
    prev = permute(flat_frame, from_frame(-1))
    nxt = permute(masked, from_frame(1))
    up_y = spread_y(up4, UP_OFFSETS)
    down_y = spread_y(down4, DOWN_OFFSETS)
    conv0 = conv(0, 3, frame, space_kernel, time_kernel, row(conv_bias))
    conv1 = conv(3, 3, frame, space_kernel, time_kernel, row(conv_bias))
    up_own = [up_y] + spread_x(up_y)
    up_other = [swap_core(block) for block in up_own]
    down_own = [down_y] + spread_x(down_y)
    down_other = [swap_core(block) for block in down_own]
    hid, energy = up(
        clip_cut,
        conv0,
        conv1,
        prev,
        nxt,
        time_kernel,
        row(norm_gain),
        row(norm_bias),
        row(up_bias),
        up_own,
        up_other,
    )
    out = down(
        hid, energy, row(grn_gamma), row(grn_beta), row(down_bias), flat_frame, down_own, down_other
    )
    return out[None]


def solution(mesh):
    return jax.shard_map(
        per_device,
        mesh=mesh,
        in_specs=(
            P(("video", "tm"), None, None, None),
            P(("video", "tm")),
            P(),
            P(),
            P(),
            P(),
            P(),
            P(None, "tm"),
            P(),
            P(),
            P(),
            P("tm", None),
            P(),
        ),
        out_specs=P(("video", "tm"), None, None, None),
        check_vma=False,
    )
```

```python
import jax
import jax.numpy as jnp
from jax import lax
from jax.experimental import pallas as pl
from jax.experimental.pallas import tpu as pltpu
from jax.sharding import PartitionSpec as P

C, HID, H, W = 704, 2816, 28, 28
PIX = H * W
LANES = 128
CHUNKS = 6
SHARD = 88
MIB = 1024 * 1024
OFFSETS = ((0, 1, 7, 2), (4, 5, 3, 6))

vmem_spec = pl.BlockSpec(memory_space=pltpu.VMEM)
smem_spec = pl.BlockSpec(memory_space=pltpu.SMEM)
hbm_spec = pl.BlockSpec(memory_space=pl.ANY)


def after(value, *first):
    return lax.optimization_barrier((value,) + first)[0]


def place():
    v = lax.axis_index("video")
    t = lax.axis_index("tm")
    return v // 4, v % 2, t // 4, t % 4


def pick(table, index):
    value = jnp.int32(table[0])
    for k in range(1, len(table)):
        value = jnp.where(index == k, jnp.int32(table[k]), value)
    return value


def permute(value, source_of):
    pairs = []
    for x in range(4):
        for zh in range(2):
            for c in range(2):
                for y in range(8):
                    for zl in range(4):
                        src = source_of(x, zh, c, y, zl)
                        if src is None:
                            continue
                        pairs.append((flat(*src), flat(x, zh, c, y, zl)))
    return lax.ppermute(value, ("video", "tm"), pairs)


def flat(x, zh, c, y, zl):
    return ((x * 2 + zh) * 2 + c) * 32 + y * 4 + zl


def from_frame(by):
    def source_of(x, zh, c, y, zl):
        t = y * 4 + zl + by
        return (x, zh, c, t // 4, t % 4) if 0 <= t < 32 else None

    return source_of


def widen(value):
    if value.shape[-1] == LANES:
        return value
    zeros = jnp.zeros(value.shape[:-1] + (LANES - value.shape[-1],), value.dtype)
    return jnp.concatenate([value, zeros], axis=-1)


def lanes(chunk):
    return slice(chunk * LANES, min((chunk + 1) * LANES, C))


def flatten_kernel(clip_ref, x_ref, flat_ref, masked_ref):
    keep = (1 - clip_ref[0]).astype(jnp.float32)
    for g in range(7):
        rows = jnp.concatenate([x_ref[4 * g + r].astype(jnp.float32) for r in range(4)], axis=0)
        flat_ref[112 * g : 112 * (g + 1), :] = rows.astype(jnp.bfloat16)
        masked_ref[112 * g : 112 * (g + 1), :] = (rows * keep).astype(jnp.bfloat16)


def flatten(clip, frame):
    out = jax.ShapeDtypeStruct((PIX, C), jnp.bfloat16)
    return pl.pallas_call(
        flatten_kernel,
        out_shape=(out, out),
        in_specs=[smem_spec, vmem_spec],
        out_specs=(vmem_spec, vmem_spec),
        compiler_params=pltpu.CompilerParams(vmem_limit_bytes=8 * MIB),
        name="flatten",
    )(clip, frame)


def conv_kernel(first, count, x_ref, k_ref, t_ref, b_ref, o_ref, xp, kb, bb):
    xp[...] = jnp.zeros_like(xp)
    for n in range(count):
        part = lanes(first + n)
        for i in range(H):
            xp[n, 3 + i, 3:31, :] = widen(x_ref[i, :, part].astype(jnp.float32))
        for tap in range(49):
            row = widen(k_ref[tap : tap + 1, part])
            if tap == 24:
                row = row + widen(t_ref[1:2, part])
            kb[n, tap] = jnp.broadcast_to(row, (8, LANES))
        bb[n] = jnp.broadcast_to(widen(b_ref[part][None]), (8, LANES))

    def body(step, carry):
        n = step // 7
        g = step % 7
        done = [[None] * 4 for _ in range(4)]
        for jb in range(4):
            acc = [bb[n]] * 4
            for b in range(7):
                xs = [xp[n, 4 * g + q, 8 * jb + b : 8 * jb + b + 8, :] for q in range(10)]
                for a in range(7):
                    kv = kb[n, 7 * a + b]
                    for r in range(4):
                        acc[r] = acc[r] + kv * xs[r + a]
            for r in range(4):
                done[r][jb] = acc[r] if jb < 3 else acc[r][:4]
        rows = jnp.concatenate([done[r][jb] for r in range(4) for jb in range(4)], axis=0)
        o_ref[n, pl.ds(pl.multiple_of(112 * g, 8), 112), :] = rows
        return carry

    lax.fori_loop(0, 7 * count, body, 0)


def conv(first, count, frame, space_kernel, time_kernel, conv_bias):
    return pl.pallas_call(
        lambda *refs: conv_kernel(first, count, *refs),
        out_shape=jax.ShapeDtypeStruct((count, PIX, LANES), jnp.float32),
        in_specs=[vmem_spec] * 4,
        out_specs=vmem_spec,
        scratch_shapes=[
            pltpu.VMEM((count, 34, 40, LANES), jnp.float32),
            pltpu.VMEM((count, 49, 8, LANES), jnp.float32),
            pltpu.VMEM((count, 8, LANES), jnp.float32),
        ],
        compiler_params=pltpu.CompilerParams(vmem_limit_bytes=14 * MIB),
        name="conv",
    )(frame, space_kernel, time_kernel, conv_bias)


def join_kernel(*refs):
    for k, source in enumerate(refs[:-1]):
        refs[-1][k] = source[...]


def join(blocks):
    shape = (len(blocks),) + blocks[0].shape
    return pl.pallas_call(
        join_kernel,
        out_shape=jax.ShapeDtypeStruct(shape, jnp.bfloat16),
        in_specs=[vmem_spec] * len(blocks),
        out_specs=vmem_spec,
        compiler_params=pltpu.CompilerParams(vmem_limit_bytes=12 * MIB),
        name="join",
    )(*blocks)


def split_kernel(*refs):
    for r in range(4):
        refs[4][r] = refs[r][0]
        refs[5][r] = refs[r][1]


def split(blocks):
    out = jax.ShapeDtypeStruct((4, SHARD, C), jnp.bfloat16)
    return pl.pallas_call(
        split_kernel,
        out_shape=(out, out),
        in_specs=[vmem_spec] * 4,
        out_specs=(vmem_spec, vmem_spec),
        compiler_params=pltpu.CompilerParams(vmem_limit_bytes=12 * MIB),
        name="split",
    )(*blocks)


def place_blocks(own, other, weight):
    x, core, y, zl = place()
    for step in range(4):
        for side, ref in ((core, own), (1 - core, other)):
            for r in range(4):
                column = (x + step + r) % 4
                offset = jnp.where(side == 0, pick(OFFSETS[0], column), pick(OFFSETS[1], column))
                row = (((y + offset) % 8) * 4 + (zl ^ r)) * SHARD
                weight[pl.ds(pl.multiple_of(row, 8), SHARD), :] = ref[step, r].astype(jnp.float32)


def up_kernel(clip_ref, *refs):
    (c0_ref, c1_ref, prev_ref, next_ref, t_ref, gain_ref, nbias_ref, ubias_ref) = refs[:8]
    own, other, hid_ref, energy_ref, weight, normed = refs[8:]
    place_blocks(own, other, weight)
    keep = (1 - clip_ref[0]).astype(jnp.float32)

    gain = [widen(gain_ref[lanes(n)][None]) for n in range(CHUNKS)]
    nbias = [widen(nbias_ref[lanes(n)][None]) for n in range(CHUNKS)]

    def norm_rows(step, carry):
        rows = pl.ds(pl.multiple_of(step * 112, 16), 112)
        parts = []
        for n in range(CHUNKS):
            part = lanes(n)
            base = c0_ref[n, rows, :] if n < 3 else c1_ref[n - 3, rows, :]
            before = widen(prev_ref[rows, part].astype(jnp.float32)) * (widen(t_ref[0:1, part]) * keep)
            after = widen(next_ref[rows, part].astype(jnp.float32)) * widen(t_ref[2:3, part])
            parts.append(base + before + after)
        total = parts[0]
        for n in range(1, CHUNKS):
            total = total + parts[n]
        mean = jnp.sum(total, axis=-1, keepdims=True) * (1.0 / C)
        parts = [p - mean for p in parts]
        lane = lax.broadcasted_iota(jnp.int32, parts[-1].shape, 1)
        parts[-1] = jnp.where(lane < C - 5 * LANES, parts[-1], 0.0)
        total = parts[0] * parts[0]
        for n in range(1, CHUNKS):
            total = total + parts[n] * parts[n]
        var = jnp.sum(total, axis=-1, keepdims=True) * (1.0 / C)
        scale = lax.rsqrt(var + 1e-06)
        for n in range(CHUNKS):
            value = parts[n] * scale * gain[n] + nbias[n]
            normed[rows, n * LANES : (n + 1) * LANES] = value.astype(jnp.bfloat16)
        return carry

    lax.fori_loop(0, PIX // 112, norm_rows, 0)

    def units(step, carry):
        cols = pl.ds(pl.multiple_of(step * 256, 256), 256)
        dims = (((1,), (1,)), ((), ()))
        value = lax.dot_general(
            normed[:, :C], weight[cols, :].astype(jnp.bfloat16), dims, preferred_element_type=jnp.float32
        )
        value = value + ubias_ref[cols][None]
        hid = (0.5 * value * (1.0 + lax.erf(value * 0.7071067811865476))).astype(jnp.bfloat16)
        hid_ref[:, cols] = hid
        wide = hid.astype(jnp.float32)
        energy_ref[:, cols] = jnp.sum(wide * wide, axis=0, keepdims=True)
        return carry

    lax.fori_loop(0, HID // 256, units, 0)


def up(clip, conv0, conv1, prev, nxt, time_kernel, gain, nbias, ubias, own, other):
    return pl.pallas_call(
        up_kernel,
        out_shape=(
            jax.ShapeDtypeStruct((PIX, HID), jnp.bfloat16),
            jax.ShapeDtypeStruct((1, HID), jnp.float32),
        ),
        in_specs=[smem_spec] + [vmem_spec] * 8 + [vmem_spec] * 2,
        out_specs=(vmem_spec, vmem_spec),
        scratch_shapes=[
            pltpu.VMEM((HID, C), jnp.float32),
            pltpu.VMEM((PIX, CHUNKS * LANES), jnp.bfloat16),
        ],
        compiler_params=pltpu.CompilerParams(vmem_limit_bytes=29 * MIB),
        name="up",
    )(clip, conv0, conv1, prev, nxt, time_kernel, gain, nbias, ubias, own, other)


def down_kernel(hid_ref, energy_ref, gamma_ref, beta_ref, dbias_ref, flat_ref, *refs):
    own, other, out_ref, weight, grn, sums = refs
    place_blocks(own, other, weight)
    energy = jnp.sqrt(energy_ref[...])
    ratio = energy / (jnp.sum(energy, axis=1, keepdims=True) * (1.0 / HID) + 1e-06)
    grow = gamma_ref[...][None] * ratio + 1.0
    beta = beta_ref[...][None]

    def scale(step, carry):
        rows = pl.ds(pl.multiple_of(step * 16, 16), 16)
        grn[rows, :] = (hid_ref[rows, :].astype(jnp.float32) * grow + beta).astype(jnp.bfloat16)
        return carry

    lax.fori_loop(0, PIX // 16, scale, 0)
    for cols in (slice(0, 256), slice(256, 512), slice(512, C)):
        sums[:, cols] = jnp.dot(grn[...], weight[:, cols].astype(jnp.bfloat16), preferred_element_type=jnp.float32)
    for g in range(7):
        rows = slice(112 * g, 112 * (g + 1))
        value = sums[rows, :] + dbias_ref[...][None] + flat_ref[rows, :].astype(jnp.float32)
        for r in range(4):
            out_ref[4 * g + r] = value[28 * r : 28 * (r + 1)].astype(jnp.bfloat16)


def down(hid, energy, gamma, beta, dbias, flat_frame, own, other):
    return pl.pallas_call(
        down_kernel,
        out_shape=jax.ShapeDtypeStruct((H, W, C), jnp.bfloat16),
        in_specs=[vmem_spec] * 6 + [vmem_spec] * 2,
        out_specs=vmem_spec,
        scratch_shapes=[
            pltpu.VMEM((HID, C), jnp.float32),
            pltpu.VMEM((PIX, HID), jnp.bfloat16),
            pltpu.VMEM((PIX, C), jnp.float32),
        ],
        compiler_params=pltpu.CompilerParams(vmem_limit_bytes=33 * MIB),
        name="down",
    )(hid, energy, gamma, beta, dbias, flat_frame, own, other)


def spread_yz(both):
    blocks = []
    for r in range(4):
        blocks.append(
            permute(
                both,
                lambda x, zh, c, y, zl: (x, zh, c, (y + OFFSETS[c][(x + r) % 4]) % 8, zl ^ r),
            )
        )
    return blocks


def from_x(block, by):
    return permute(block, lambda x, zh, c, y, zl: ((x + by) % 4, zh, c, y, zl))


def swap_core(block):
    return permute(block, lambda x, zh, c, y, zl: (x, zh, 1 - c, y, zl))


def per_device(
    frames,
    clip_cut,
    space_kernel,
    time_kernel,
    conv_bias,
    norm_gain,
    norm_bias,
    up_weight,
    up_bias,
    grn_gamma,
    grn_beta,
    down_weight,
    down_bias,
):
    frame = frames[0]
    both = jnp.stack([up_weight.T, down_weight])
    blocks = spread_yz(both)
    conv0 = conv(0, 3, frame, space_kernel, time_kernel, conv_bias)
    flat_frame, masked = flatten(clip_cut, frame)
    blocks = [after(block, flat_frame, conv0) for block in blocks]
    prev = permute(after(flat_frame, *blocks), from_frame(-1))
    nxt = permute(after(masked, *blocks), from_frame(1))
    up_yz, down_yz = split(blocks)
    conv1 = conv(3, 3, frame, space_kernel, time_kernel, after(conv_bias, up_yz))
    up_1 = from_x(up_yz, 1)
    up_3 = from_x(up_yz, 3)
    down_3 = from_x(down_yz, 3)
    down_1 = from_x(after(down_yz, conv1, up_1), 1)
    up_2 = from_x(after(up_1, conv1), 1)
    down_2 = from_x(after(down_3, up_3), 3)
    up_own = join([after(block, prev) for block in (up_yz, up_1, up_2, up_3)])
    up_other = swap_core(up_own)
    down_own = join([after(block, nxt) for block in (down_yz, down_1, down_2, down_3)])
    down_other = swap_core(down_own)
    hid, energy = up(
        clip_cut,
        conv0,
        conv1,
        prev,
        nxt,
        time_kernel,
        norm_gain,
        norm_bias,
        up_bias,
        up_own,
        up_other,
    )
    out = down(
        hid, energy, grn_gamma, grn_beta, down_bias, flat_frame, down_own, down_other
    )
    return out[None]


def solution(mesh):
    return jax.shard_map(
        per_device,
        mesh=mesh,
        in_specs=(
            P(("video", "tm"), None, None, None),
            P(("video", "tm")),
            P(),
            P(),
            P(),
            P(),
            P(),
            P(None, "tm"),
            P(),
            P(),
            P(),
            P("tm", None),
            P(),
        ),
        out_specs=P(("video", "tm"), None, None, None),
        check_vma=False,
    )
```

```python
import functools

import jax
import jax.numpy as jnp
from jax import lax
from jax.experimental import pallas as pl
from jax.experimental.pallas import tpu as pltpu
from jax.sharding import PartitionSpec as P

C, HID, H, W = 704, 2816, 28, 28
PIX = H * W
LANES = 128
CHUNKS = 6
LOW = 400
TAIL = C - (CHUNKS - 1) * LANES
SENT = (CHUNKS - 1) * PIX + LOW
SHARD = 88
MIB = 1024 * 1024
OFFSETS = ((0, 1, 7, 2), (4, 5, 3, 6))

vmem_spec = pl.BlockSpec(memory_space=pltpu.VMEM)
smem_spec = pl.BlockSpec(memory_space=pltpu.SMEM)
hbm_spec = pl.BlockSpec(memory_space=pl.ANY)


def after(value, *first):
    return lax.optimization_barrier((value,) + first)[0]


def place():
    v = lax.axis_index("video")
    t = lax.axis_index("tm")
    return v // 4, v % 2, t // 4, t % 4


def pick(table, index):
    value = jnp.int32(table[0])
    for k in range(1, len(table)):
        value = jnp.where(index == k, jnp.int32(table[k]), value)
    return value


def permute(value, source_of):
    pairs = []
    for x in range(4):
        for zh in range(2):
            for c in range(2):
                for y in range(8):
                    for zl in range(4):
                        src = source_of(x, zh, c, y, zl)
                        if src is None:
                            continue
                        pairs.append((flat(*src), flat(x, zh, c, y, zl)))
    return lax.ppermute(value, ("video", "tm"), pairs)


def flat(x, zh, c, y, zl):
    return ((x * 2 + zh) * 2 + c) * 32 + y * 4 + zl


def from_frame(by):
    def source_of(x, zh, c, y, zl):
        t = y * 4 + zl + by
        return (x, zh, c, t // 4, t % 4) if 0 <= t < 32 else None

    return source_of


def widen(value):
    if value.shape[-1] == LANES:
        return value
    zeros = jnp.zeros(value.shape[:-1] + (LANES - value.shape[-1],), value.dtype)
    return jnp.concatenate([value, zeros], axis=-1)


def sent_chunk(ref, n, first, offset, count):
    if n < CHUNKS - 1:
        return ref[pl.ds(pl.multiple_of(n * PIX + first + offset, 16), count), :].astype(jnp.float32)
    rows = pl.ds(pl.multiple_of(n * PIX + offset, 16), count)
    part = slice(0, TAIL) if first < LOW else slice(TAIL, LANES)
    return widen(ref[rows, part].astype(jnp.float32))


def lanes(chunk):
    return slice(chunk * LANES, min((chunk + 1) * LANES, C))


def flatten_kernel(clip_ref, x_ref, flat_ref, plain_ref, masked_ref):
    keep = (1 - clip_ref[0]).astype(jnp.float32)

    def put(first, rows):
        count = rows.shape[0]
        for n in range(CHUNKS):
            part, start = slice(0, LANES), n * PIX + first
            if n == CHUNKS - 1:
                part = slice(0, TAIL) if first < LOW else slice(TAIL, LANES)
                start = start if first < LOW else start - LOW
            value = rows[:, lanes(n)]
            plain_ref[start : start + count, part] = value.astype(jnp.bfloat16)
            masked_ref[start : start + count, part] = (value * keep).astype(jnp.bfloat16)

    for g in range(7):
        rows = jnp.concatenate([x_ref[4 * g + r].astype(jnp.float32) for r in range(4)], axis=0)
        flat_ref[112 * g : 112 * (g + 1), :] = rows.astype(jnp.bfloat16)
        cut = LOW - 112 * g
        if 0 < cut < 112:
            put(112 * g, rows[:cut])
            put(LOW, rows[cut:])
        else:
            put(112 * g, rows)
    blank = jnp.zeros((2 * LOW - PIX, LANES - TAIL), jnp.bfloat16)
    plain_ref[SENT - (2 * LOW - PIX) :, TAIL:] = blank
    masked_ref[SENT - (2 * LOW - PIX) :, TAIL:] = blank


def flatten(clip, frame):
    flat_shape = jax.ShapeDtypeStruct((PIX, C), jnp.bfloat16)
    packed = jax.ShapeDtypeStruct((SENT, LANES), jnp.bfloat16)
    return pl.pallas_call(
        flatten_kernel,
        out_shape=(flat_shape, packed, packed),
        in_specs=[smem_spec, vmem_spec],
        out_specs=(vmem_spec, vmem_spec, vmem_spec),
        compiler_params=pltpu.CompilerParams(vmem_limit_bytes=12 * MIB),
        name="flatten",
    )(clip, frame)


def conv_kernel(first, count, x_ref, k_ref, t_ref, b_ref, o_ref, xp, kb, bb):
    xp[...] = jnp.zeros_like(xp)
    for n in range(count):
        part = lanes(first + n)
        for i in range(H):
            xp[n, 3 + i, 3:31, :] = widen(x_ref[i, :, part].astype(jnp.float32))
        for tap in range(49):
            row = widen(k_ref[tap : tap + 1, part])
            if tap == 24:
                row = row + widen(t_ref[1:2, part])
            kb[n, tap] = jnp.broadcast_to(row, (8, LANES))
        bb[n] = jnp.broadcast_to(widen(b_ref[part][None]), (8, LANES))

    def body(step, carry):
        n = step // 7
        g = step % 7
        done = [[None] * 4 for _ in range(4)]
        for jb in range(4):
            acc = [bb[n]] * 4
            for b in range(7):
                xs = [xp[n, 4 * g + q, 8 * jb + b : 8 * jb + b + 8, :] for q in range(10)]
                for a in range(7):
                    kv = kb[n, 7 * a + b]
                    for r in range(4):
                        acc[r] = acc[r] + kv * xs[r + a]
            for r in range(4):
                done[r][jb] = acc[r] if jb < 3 else acc[r][:4]
        rows = jnp.concatenate([done[r][jb] for r in range(4) for jb in range(4)], axis=0)
        o_ref[n, pl.ds(pl.multiple_of(112 * g, 8), 112), :] = rows
        return carry

    lax.fori_loop(0, 7 * count, body, 0)


def conv(first, count, frame, space_kernel, time_kernel, conv_bias):
    return pl.pallas_call(
        lambda *refs: conv_kernel(first, count, *refs),
        out_shape=jax.ShapeDtypeStruct((count, PIX, LANES), jnp.float32),
        in_specs=[vmem_spec] * 4,
        out_specs=vmem_spec,
        scratch_shapes=[
            pltpu.VMEM((count, 34, 40, LANES), jnp.float32),
            pltpu.VMEM((count, 49, 8, LANES), jnp.float32),
            pltpu.VMEM((count, 8, LANES), jnp.float32),
        ],
        compiler_params=pltpu.CompilerParams(vmem_limit_bytes=14 * MIB),
        name="conv",
    )(frame, space_kernel, time_kernel, conv_bias)


def join_kernel(*refs):
    for k, source in enumerate(refs[:-1]):
        refs[-1][k] = source[...]


def join(blocks):
    shape = (len(blocks),) + blocks[0].shape
    return pl.pallas_call(
        join_kernel,
        out_shape=jax.ShapeDtypeStruct(shape, jnp.bfloat16),
        in_specs=[vmem_spec] * len(blocks),
        out_specs=vmem_spec,
        compiler_params=pltpu.CompilerParams(vmem_limit_bytes=12 * MIB),
        name="join",
    )(*blocks)


def split_kernel(*refs):
    for r in range(4):
        refs[4][r] = refs[r][0]
        refs[5][r] = refs[r][1]


def split(blocks):
    out = jax.ShapeDtypeStruct((4, SHARD, C), jnp.bfloat16)
    return pl.pallas_call(
        split_kernel,
        out_shape=(out, out),
        in_specs=[vmem_spec] * 4,
        out_specs=(vmem_spec, vmem_spec),
        compiler_params=pltpu.CompilerParams(vmem_limit_bytes=12 * MIB),
        name="split",
    )(*blocks)


def place_blocks(own, other, weight):
    x, core, y, zl = place()
    for step in range(4):
        for side, ref in ((core, own), (1 - core, other)):
            for r in range(4):
                column = (x + step + r) % 4
                offset = jnp.where(side == 0, pick(OFFSETS[0], column), pick(OFFSETS[1], column))
                row = (((y + offset) % 8) * 4 + (zl ^ r)) * SHARD
                weight[pl.ds(pl.multiple_of(row, 8), SHARD), :] = ref[step, r].astype(jnp.float32)


def up_kernel(clip_ref, *refs):
    (c0_ref, c1_ref, prev_ref, next_ref, t_ref, gain_ref, nbias_ref, ubias_ref) = refs[:8]
    own, other, hid_ref, energy_ref, weight, normed = refs[8:]
    place_blocks(own, other, weight)
    keep = (1 - clip_ref[0]).astype(jnp.float32)

    gain = [widen(gain_ref[lanes(n)][None]) for n in range(CHUNKS)]
    nbias = [widen(nbias_ref[lanes(n)][None]) for n in range(CHUNKS)]

    def norm_rows(first, count, step, carry):
        rows = pl.ds(pl.multiple_of(first + step * count, 16), count)
        parts = []
        for n in range(CHUNKS):
            part = lanes(n)
            base = c0_ref[n, rows, :] if n < 3 else c1_ref[n - 3, rows, :]
            before = sent_chunk(prev_ref, n, first, step * count, count) * (widen(t_ref[0:1, part]) * keep)
            after = sent_chunk(next_ref, n, first, step * count, count) * widen(t_ref[2:3, part])
            parts.append(base + before + after)
        total = parts[0]
        for n in range(1, CHUNKS):
            total = total + parts[n]
        mean = jnp.sum(total, axis=-1, keepdims=True) * (1.0 / C)
        parts = [p - mean for p in parts]
        lane = lax.broadcasted_iota(jnp.int32, parts[-1].shape, 1)
        parts[-1] = jnp.where(lane < C - 5 * LANES, parts[-1], 0.0)
        total = parts[0] * parts[0]
        for n in range(1, CHUNKS):
            total = total + parts[n] * parts[n]
        var = jnp.sum(total, axis=-1, keepdims=True) * (1.0 / C)
        scale = lax.rsqrt(var + 1e-06)
        for n in range(CHUNKS):
            value = parts[n] * scale * gain[n] + nbias[n]
            normed[rows, n * LANES : (n + 1) * LANES] = value.astype(jnp.bfloat16)
        return carry

    lax.fori_loop(0, 5, functools.partial(norm_rows, 0, 80), 0)
    lax.fori_loop(0, 4, functools.partial(norm_rows, LOW, 96), 0)

    def units(step, carry):
        cols = pl.ds(pl.multiple_of(step * 256, 256), 256)
        dims = (((1,), (1,)), ((), ()))
        value = lax.dot_general(
            normed[:, :C], weight[cols, :].astype(jnp.bfloat16), dims, preferred_element_type=jnp.float32
        )
        value = value + ubias_ref[cols][None]
        hid = (0.5 * value * (1.0 + lax.erf(value * 0.7071067811865476))).astype(jnp.bfloat16)
        hid_ref[:, cols] = hid
        wide = hid.astype(jnp.float32)
        energy_ref[:, cols] = jnp.sum(wide * wide, axis=0, keepdims=True)
        return carry

    lax.fori_loop(0, HID // 256, units, 0)


def up(clip, conv0, conv1, prev, nxt, time_kernel, gain, nbias, ubias, own, other):
    return pl.pallas_call(
        up_kernel,
        out_shape=(
            jax.ShapeDtypeStruct((PIX, HID), jnp.bfloat16),
            jax.ShapeDtypeStruct((1, HID), jnp.float32),
        ),
        in_specs=[smem_spec] + [vmem_spec] * 8 + [vmem_spec] * 2,
        out_specs=(vmem_spec, vmem_spec),
        scratch_shapes=[
            pltpu.VMEM((HID, C), jnp.float32),
            pltpu.VMEM((PIX, CHUNKS * LANES), jnp.bfloat16),
        ],
        compiler_params=pltpu.CompilerParams(vmem_limit_bytes=29 * MIB),
        name="up",
    )(clip, conv0, conv1, prev, nxt, time_kernel, gain, nbias, ubias, own, other)


def down_kernel(hid_ref, energy_ref, gamma_ref, beta_ref, dbias_ref, flat_ref, *refs):
    own, other, out_ref, weight, grn, sums = refs
    place_blocks(own, other, weight)
    energy = jnp.sqrt(energy_ref[...])
    ratio = energy / (jnp.sum(energy, axis=1, keepdims=True) * (1.0 / HID) + 1e-06)
    grow = gamma_ref[...][None] * ratio + 1.0
    beta = beta_ref[...][None]

    def scale(step, carry):
        rows = pl.ds(pl.multiple_of(step * 16, 16), 16)
        grn[rows, :] = (hid_ref[rows, :].astype(jnp.float32) * grow + beta).astype(jnp.bfloat16)
        return carry

    lax.fori_loop(0, PIX // 16, scale, 0)
    for cols in (slice(0, 256), slice(256, 512), slice(512, C)):
        sums[:, cols] = jnp.dot(grn[...], weight[:, cols].astype(jnp.bfloat16), preferred_element_type=jnp.float32)
    for g in range(7):
        rows = slice(112 * g, 112 * (g + 1))
        value = sums[rows, :] + dbias_ref[...][None] + flat_ref[rows, :].astype(jnp.float32)
        for r in range(4):
            out_ref[4 * g + r] = value[28 * r : 28 * (r + 1)].astype(jnp.bfloat16)


def down(hid, energy, gamma, beta, dbias, flat_frame, own, other):
    return pl.pallas_call(
        down_kernel,
        out_shape=jax.ShapeDtypeStruct((H, W, C), jnp.bfloat16),
        in_specs=[vmem_spec] * 6 + [vmem_spec] * 2,
        out_specs=vmem_spec,
        scratch_shapes=[
            pltpu.VMEM((HID, C), jnp.float32),
            pltpu.VMEM((PIX, HID), jnp.bfloat16),
            pltpu.VMEM((PIX, C), jnp.float32),
        ],
        compiler_params=pltpu.CompilerParams(vmem_limit_bytes=33 * MIB),
        name="down",
    )(hid, energy, gamma, beta, dbias, flat_frame, own, other)


def spread_yz(both):
    blocks = []
    for r in range(4):
        blocks.append(
            permute(
                both,
                lambda x, zh, c, y, zl: (x, zh, c, (y + OFFSETS[c][(x + r) % 4]) % 8, zl ^ r),
            )
        )
    return blocks


def from_x(block, by):
    return permute(block, lambda x, zh, c, y, zl: ((x + by) % 4, zh, c, y, zl))


def swap_core(block):
    return permute(block, lambda x, zh, c, y, zl: (x, zh, 1 - c, y, zl))


def per_device(
    frames,
    clip_cut,
    space_kernel,
    time_kernel,
    conv_bias,
    norm_gain,
    norm_bias,
    up_weight,
    up_bias,
    grn_gamma,
    grn_beta,
    down_weight,
    down_bias,
):
    frame = frames[0]
    both = jnp.stack([up_weight.T, down_weight])
    blocks = spread_yz(both)
    conv0 = conv(0, 3, frame, space_kernel, time_kernel, conv_bias)
    flat_frame, plain, masked = flatten(clip_cut, frame)
    blocks = [after(block, flat_frame, conv0) for block in blocks]
    prev = permute(after(plain, *blocks), from_frame(-1))
    nxt = permute(after(masked, *blocks), from_frame(1))
    up_yz, down_yz = split(blocks)
    conv1 = conv(3, 3, frame, space_kernel, time_kernel, after(conv_bias, up_yz))
    up_1 = from_x(up_yz, 1)
    up_3 = from_x(up_yz, 3)
    down_3 = from_x(down_yz, 3)
    down_1 = from_x(after(down_yz, conv1, up_1), 1)
    up_2 = from_x(after(up_1, conv1), 1)
    down_2 = from_x(after(down_3, up_3), 3)
    up_own = join([up_yz, up_1, up_2, up_3])
    up_other = swap_core(up_own)
    down_own = join([after(block, prev, nxt) for block in (down_yz, down_1, down_2, down_3)])
    down_other = swap_core(down_own)
    hid, energy = up(
        clip_cut,
        conv0,
        conv1,
        prev,
        nxt,
        time_kernel,
        norm_gain,
        norm_bias,
        up_bias,
        up_own,
        up_other,
    )
    out = down(
        hid, energy, grn_gamma, grn_beta, down_bias, flat_frame, down_own, down_other
    )
    return out[None]


def solution(mesh):
    return jax.shard_map(
        per_device,
        mesh=mesh,
        in_specs=(
            P(("video", "tm"), None, None, None),
            P(("video", "tm")),
            P(),
            P(),
            P(),
            P(),
            P(),
            P(None, "tm"),
            P(),
            P(),
            P(),
            P("tm", None),
            P(),
        ),
        out_specs=P(("video", "tm"), None, None, None),
        check_vma=False,
    )
```
